32 devices in a mesh: bulk: 4 (over z), expert: 8 (over y, x, core).
Axes of the slice: x: 2, y: 2, z: 4, core: 2. Of those that a mesh axis runs over, the one named last changes fastest.
Arguments:
- tokens: bfloat16 [2048, 7168], P(('bulk', 'expert')), may hold values from -6 to 6
- expert_ids: int32 [2048, 8], P(('bulk', 'expert')), may hold values from 0 to 255, all different within a row; in each aligned block of 64 rows (0 to 63, 64 to 127, ...) at most 3 rows name the same one
- gate_values: float32 [2048, 8], P(('bulk', 'expert')), may hold values from 0.25 to 2.5
- placement: int32 [8], replicated, may hold values from 0 to 7, as said below
- gate_weight: bfloat16 [8, 7168, 2048], P('expert', 'bulk'), may hold values from -0.0625 to 0.0625
- up_weight: bfloat16 [8, 7168, 2048], P('expert', 'bulk'), may hold values from -0.0625 to 0.0625
- down_weight: bfloat16 [8, 2048, 7168], P('expert', None, 'bulk'), may hold values from -0.125 to 0.125
Outputs:
- layer_out: bfloat16 [2048, 7168], P(('bulk', 'expert'))
- host_load: int32 [32, 8], P(('bulk', 'expert'))
The draws below stay inside these ranges and needn't reach their ends.
Inputs may be any that keep to these rules, and one draw needn't show every extreme that they name: `expert_ids`: in each aligned block of 64 rows (the tokens of one device) no expert is named by more than 3 rows; a token names an expert at most once. Exactly one expert e has placement[e] != e: its home device e is power-capped and its host is the next device of the expert axis, placement[e] = (e + 1) mod 8; every other expert stays on its home device.
All inputs are finite; a program needn't handle non-finite values.
Results may differ from the reference program's by a relative error of at most 0.018.
Values may be sent and summed in bfloat16 or wider, within the bound.
A program may use at most 128 MiB of HBM per device.

```python
import math
import jax
import jax.numpy as jnp
import numpy as np
from jax import lax

D = 7168
FF = 2048
EXPERTS = 256
TOP = 8
TOK_DEV = 64
CAP = 3
IN_FLIGHT = 8
SOURCES = 32
TOKENS = 2048
N_BULK = 4


def draw_placement(key, part):
    home_device = jnp.arange(IN_FLIGHT, dtype=jnp.int32)
    removed_device = jax.random.randint(jax.random.fold_in(key, 11), (), 0, IN_FLIGHT)
    host_device = (removed_device + 1) % IN_FLIGHT
    return jnp.where(home_device == removed_device, host_device, home_device).astype(jnp.int32)


def steps_of(rng, shape, cuts, least, top_value):
    loudness = 1.0
    for axis_at, parts in cuts:
        draws = jax.random.uniform(jax.random.fold_in(jax.random.fold_in(rng, 6), axis_at), (parts,), jnp.float32, least / len(cuts), top_value / len(cuts))
        loudness = loudness * jnp.repeat(jnp.exp(draws), shape[axis_at] // parts).reshape((-1,) + (1,) * (len(shape) - 1 - axis_at))
    return loudness


def deal_out(own_key, own, number, rows, count, top, limit, lean):
    ranking = jax.random.permutation(own_key, count)
    packed, ordinary = portions_of(count, rows * top, limit, lean, True), portions_of(count, rows * top, limit, lean, False)
    places = jnp.arange(count)

    def named(tallies, offset_by):
        used = int((tallies > 0).sum())
        fixed = max(1, used // 4)
        moved = fixed + (places - fixed + offset_by * (used - fixed)) % max(1, count - fixed)
        return jnp.zeros((count,), jnp.int32).at[ranking[jnp.where(places < fixed, places, moved)]].set(jnp.asarray(tallies, jnp.int32))

    tallies = jnp.where(number % 4 == 0, named(packed, number // 4), named(ordinary, number - number // 4 - 1))
    mixed = jax.random.permutation(jax.random.fold_in(own, 3), count)
    giver, receiver = mixed[0:count // 2 * 2:2], mixed[1:count // 2 * 2:2]
    margin = jnp.minimum(tallies[giver] - 1, limit - tallies[receiver]) // 2
    margin = jnp.where((giver == ranking[0]) | (receiver == ranking[0]) | (tallies[receiver] == 0), 0, jnp.maximum(margin, 0))
    moved = jax.random.randint(jax.random.fold_in(own, 4), (count // 2,), 0, 1 << 20) % (margin + 1)
    tallies = tallies.at[giver].add(-moved).at[receiver].add(moved)
    labels = jnp.searchsorted(jnp.cumsum(tallies), jnp.arange(rows * top), side="right").astype(jnp.int32)
    table = labels.reshape(top, rows).T
    table = table[jax.random.permutation(jax.random.fold_in(own, 1), rows)]
    offset_by = jax.random.randint(jax.random.fold_in(own, 2), (rows, 1), 0, top)
    return jnp.take_along_axis(table, (jnp.arange(top)[None, :] + offset_by) % top, axis=1)


def portions_of(count, total, reach, skew, full):
    portions = [(1 << 20) // math.isqrt(standing ** skew) + 1 for standing in range(1, count + 1)]
    largest = reach if full else min(reach, max(-(-total // count), total * portions[0] // sum(portions)))
    least = 1 if total - largest >= count - 1 else 0
    counts, spare = [largest] + [least] * (count - 1), total - largest - least * (count - 1)
    while spare > 0:
        free = [i for i in range(1, count) if counts[i] < largest] or [i for i in range(1, count) if counts[i] < reach]
        pool, remaining = sum([portions[i] for i in free]), spare
        for i in free:
            more = min(reach - counts[i], max(1, remaining * portions[i] // pool), spare)
            counts[i] = counts[i] + more
            spare = spare - more
    return np.array(counts)


def bell_draw(stream_key, extent, spread, reach, cuts=(), held_as=jnp.bfloat16):
    values = spread * jax.random.normal(stream_key, extent, jnp.float32)
    if cuts:
        values = values * steps_of(stream_key, extent, cuts, -0.22, 0.18)
    return jnp.clip(values, -reach, reach).astype(held_as)


def setup_inputs(seed: int = 0) -> dict:
    key_of = jax.random.split(jax.random.key(seed), 8)
    tokens = bell_draw(key_of[0], (TOKENS, D), 1.0, 6.0, ((0, 32),))
    expert_ids_keys = jax.random.split(jax.random.fold_in(key_of[1], 1), TOKENS // TOK_DEV)
    expert_ids_turns = jax.random.permutation(jax.random.fold_in(key_of[1], 3), TOKENS // TOK_DEV)
    expert_ids = jax.vmap(lambda own, number: deal_out(jax.random.fold_in(key_of[1], 2), own, number, TOK_DEV, EXPERTS, TOP, CAP, 1))(expert_ids_keys, expert_ids_turns).reshape((TOKENS, TOP))
    gate_values = jnp.clip(0.25 + 2.25 * jax.random.uniform(key_of[2], (TOKENS, TOP), jnp.float32) ** steps_of(key_of[2], (TOKENS, TOP), ((0, 32),), -0.2, 0.2), 0.25, 2.5)
    placement = draw_placement(jax.random.fold_in(key_of[7], 71), 0)
    gate_weight = bell_draw(key_of[4], (IN_FLIGHT, D, FF), D ** -0.5, 0.0625, ((0, 8), (1, 4)))
    up_weight = bell_draw(key_of[5], (IN_FLIGHT, D, FF), D ** -0.5, 0.0625, ((0, 8), (1, 4)))
    down_weight = bell_draw(key_of[6], (IN_FLIGHT, FF, D), FF ** -0.5, 0.125, ((0, 8), (2, 4)))
    return {"tokens": tokens, "expert_ids": expert_ids, "gate_values": gate_values, "placement": placement, "gate_weight": gate_weight, "up_weight": up_weight, "down_weight": down_weight}


def reference(tokens, expert_ids, gate_values, placement, gate_weight, up_weight, down_weight):
    slice_width = D // N_BULK
    bound = SOURCES * CAP

    def step(running, inputs_now):
        expert, w_gate_now, w_up_now, w_down_now = inputs_now
        is_named_pair = expert_ids == expert
        is_named = jnp.any(is_named_pair, axis=1)
        pair_weight = jnp.sum(jnp.where(is_named_pair, gate_values, 0.0), axis=1)
        row_index = jnp.nonzero(is_named, size=bound, fill_value=0)[0].astype(jnp.int32)
        is_valid = jnp.arange(bound, dtype=jnp.int32) < jnp.sum(is_named.astype(jnp.int32))
        features = tokens[row_index].astype(jnp.float32).reshape(bound, N_BULK, slice_width)
        gate_blocks = jnp.einsum("nbd,bdf->nbf", features, w_gate_now.astype(jnp.float32).reshape(N_BULK, slice_width, FF))
        up_blocks = jnp.einsum("nbd,bdf->nbf", features, w_up_now.astype(jnp.float32).reshape(N_BULK, slice_width, FF))
        gate_rounded = lax.optimization_barrier(gate_blocks.astype(jnp.bfloat16))
        up_rounded = lax.optimization_barrier(up_blocks.astype(jnp.bfloat16))
        gate_sum = jnp.sum(gate_rounded.astype(jnp.float32), axis=1)
        up_sum = jnp.sum(up_rounded.astype(jnp.float32), axis=1)
        hidden = (jax.nn.silu(gate_sum) * up_sum).astype(jnp.bfloat16)
        expert_out = jnp.dot(hidden, w_down_now, preferred_element_type=jnp.float32).astype(jnp.bfloat16)
        pair_scale = jnp.where(is_valid, pair_weight[row_index], 0.0)
        running = running.at[row_index].add(pair_scale[:, None] * expert_out.astype(jnp.float32))
        return running, None

    start_sum = jnp.zeros((TOKENS, D), jnp.float32)
    expert_range = jnp.arange(IN_FLIGHT, dtype=jnp.int32)
    running, _ = lax.scan(step, start_sum, (expert_range, gate_weight, up_weight, down_weight))
    layer_out = running.astype(jnp.bfloat16)

    block_ids = expert_ids.reshape(SOURCES, TOK_DEV * TOP)
    block_live = block_ids < IN_FLIGHT
    safe_ids = jnp.where(block_live, block_ids, 0)
    row_within = (jnp.arange(TOK_DEV * TOP, dtype=jnp.int32) // TOP)[None, :]
    replica = (safe_ids + 1) % IN_FLIGHT
    destination = jnp.where(row_within % 2 == 1, replica, placement[safe_ids]).astype(jnp.int32)
    matches = (destination[:, :, None] == expert_range[None, None, :]) & block_live[:, :, None]
    host_load = jnp.sum(matches.astype(jnp.int32), axis=1)
    return layer_out, host_load
```

```python
import jax
import jax.numpy as jnp
from jax import lax
from jax.sharding import PartitionSpec as P

CAP = 3


def passed_along(value, axis, by):
    devices = lax.axis_size(axis)
    return lax.ppermute(value, axis, [(i, (i + by) % devices) for i in range(devices)])


def gather_rows(tokens, slot_of_pair, slot_count, tok_rows, top_count):
    selector = (jnp.arange(slot_count, dtype=jnp.int32)[:, None] == slot_of_pair[None, :]).astype(
        jnp.bfloat16
    )
    selector = jnp.sum(selector.reshape(slot_count, tok_rows, top_count), axis=2)
    return jnp.dot(selector, tokens, preferred_element_type=jnp.float32).astype(jnp.bfloat16)


def expert_rows(grouped, weight_blocks, hidden_width):
    bulk_count, per_group, slice_width = grouped.shape
    pieces = []
    offset = 0
    for partial_block_rows, partial_weights_now in weight_blocks:
        block_input = grouped[:, offset : offset + partial_block_rows]
        offset += partial_block_rows
        gate_part = jnp.einsum(
            "grd,df->grf", block_input, partial_weights_now[0], preferred_element_type=jnp.float32
        )
        up_part = jnp.einsum(
            "grd,df->grf", block_input, partial_weights_now[1], preferred_element_type=jnp.float32
        )
        pieces.append(jnp.concatenate([gate_part, up_part], axis=2))
    summed = lax.psum_scatter(
        jnp.concatenate(pieces, axis=1)
        .reshape(per_group * lax.axis_size("bulk"), 2 * hidden_width)
        .astype(jnp.bfloat16),
        "bulk",
        scatter_dimension=0,
        tiled=True,
    ).astype(jnp.float32)
    hidden = (jax.nn.silu(summed[:, :hidden_width]) * summed[:, hidden_width:]).astype(jnp.bfloat16)
    all_hidden = lax.all_gather(hidden, "bulk", axis=0, tiled=True).reshape(
        bulk_count, per_group, hidden_width
    )
    outputs = []
    offset = 0
    for block_rows, weights_now in weight_blocks:
        block_hidden = all_hidden[:, offset : offset + block_rows]
        offset += block_rows
        outputs.append(
            jnp.einsum(
                "grf,fd->grd", block_hidden, weights_now[2], preferred_element_type=jnp.float32
            ).astype(jnp.bfloat16)
        )
    return jnp.concatenate(outputs, axis=1)


def on_device(tokens, expert_ids, gate_values, placement, gate_weight, up_weight, down_weight):
    expert_count = lax.axis_size("expert")
    bulk_count = lax.axis_size("bulk")
    tok_rows, top_count = expert_ids.shape
    model_width = tokens.shape[1]
    slice_width = model_width // bulk_count
    hidden_width = gate_weight.shape[2]
    pair_count = tok_rows * top_count
    slot_count = expert_count * CAP
    expert_iota = jnp.arange(expert_count, dtype=jnp.int32)
    is_moved = placement != expert_iota
    flat_ids = expert_ids.reshape(pair_count)
    flat_gates = gate_values.reshape(pair_count)
    is_live = flat_ids < expert_count
    safe_ids = jnp.where(is_live, flat_ids, 0)
    membership = ((safe_ids[:, None] == expert_iota[None, :]) & is_live[:, None]).astype(jnp.int32)
    rank_table = jnp.cumsum(membership, axis=0) - 1
    position = jnp.sum(rank_table * membership, axis=1)
    row_within = jnp.arange(pair_count, dtype=jnp.int32) // top_count
    moved_pair = jnp.sum(membership * is_moved.astype(jnp.int32)[None, :], axis=1) > 0
    replica_dev = (safe_ids + 1) % expert_count
    to_replica = is_live & (moved_pair | (row_within % 2 == 1))
    destination = jnp.where(to_replica, replica_dev, safe_ids)
    load_table = jnp.sum(
        ((destination[:, None] == expert_iota[None, :]) & is_live[:, None]).astype(jnp.int32),
        axis=0,
    )[None, :]
    own_weights = (gate_weight[0], up_weight[0], down_weight[0])
    spread_slot = jnp.where(is_live, safe_ids * CAP + position, -1)
    kind_count = 1
    outgoing = gather_rows(tokens, spread_slot, kind_count * slot_count, tok_rows, top_count)
    outgoing = outgoing.reshape(kind_count, expert_count, CAP, model_width)
    arrived = lax.all_to_all(
        lax.all_to_all(outgoing, "bulk", split_axis=3, concat_axis=0, tiled=True),
        "expert",
        split_axis=1,
        concat_axis=1,
        tiled=True,
    )
    grouped = arrived.reshape(bulk_count, kind_count * slot_count, slice_width)
    weight_blocks = ((slot_count, own_weights),)
    results = expert_rows(grouped, weight_blocks, hidden_width)
    main_part = results.reshape(bulk_count * kind_count, expert_count, CAP, slice_width)
    returned = lax.all_to_all(
        lax.all_to_all(main_part, "bulk", split_axis=0, concat_axis=3, tiled=True),
        "expert",
        split_axis=1,
        concat_axis=1,
        tiled=True,
    )
    returned = returned.reshape(kind_count * slot_count, model_width)
    picked = jnp.take(returned, jnp.maximum(spread_slot, 0), axis=0)
    pair_scale = jnp.where(is_live, flat_gates, 0.0)
    weighted = picked.astype(jnp.float32) * pair_scale[:, None]
    layer_out = jnp.sum(weighted.reshape(tok_rows, top_count, model_width), axis=1).astype(
        jnp.bfloat16
    )
    return (layer_out, load_table)


def solution(mesh):
    placed = (
        P(("bulk", "expert"), None),
        P(("bulk", "expert"), None),
        P(("bulk", "expert"), None),
        P(),
        P("expert", "bulk", None),
        P("expert", "bulk", None),
        P("expert", None, "bulk"),
    )
    return jax.shard_map(
        on_device,
        mesh=mesh,
        in_specs=placed,
        out_specs=(P(("bulk", "expert"), None), P(("bulk", "expert"), None)),
        check_vma=False,
    )
```

```python
import functools

import jax
import jax.numpy as jnp
import ml_dtypes
import numpy as np
from jax import lax
from jax.experimental import pallas as pl
from jax.experimental.pallas import tpu as pltpu
from jax.sharding import PartitionSpec as P

CAP = 3
BF = jnp.bfloat16
F32 = jnp.float32
MESH = pl.DeviceIdType.MESH


def dot(a, b):
    return jnp.dot(a, b, preferred_element_type=F32)


def kernel(
    B, E, RP, tok, ids, gv, place, p1, p1t, p2, p2t, wg_hbm, wu_hbm, wd_hbm, out, load,
    wg, wu, wd, og, oin, xs, xr, x, pout, pin, hin, acc, back, rb, fin,
    wsem, s1, r1, s2, r2, s3, r3, s4, r4, s5, r5, s6, r6,
):
    T, TOP = ids.shape
    SL = E * CAP
    DS = wg_hbm.shape[1]
    FB = wg_hbm.shape[2] // B
    mb = lax.axis_index("bulk")
    me = lax.axis_index("expert")

    def bulk_at(k):
        return lax.rem(mb + k + B, B)

    def expert_at(k):
        return lax.rem(me + k + E, E)

    def weight_copy(i, k):
        if i == 2:
            rows = pl.ds(pl.multiple_of(bulk_at(-k) * FB, FB), FB)
            return pltpu.make_async_copy(wd_hbm.at[0, rows, :], wd.at[k], wsem.at[2, k])
        cols = pl.ds(pl.multiple_of(bulk_at(k) * FB, FB), FB)
        source, to = ((wg_hbm, wg), (wu_hbm, wu))[i]
        return pltpu.make_async_copy(source.at[0, :, cols], to.at[k], wsem.at[i, k])

    order = list(range(1, B)) + [0]
    barrier = pltpu.get_barrier_semaphore()
    for k in range(1, B):
        pl.semaphore_signal(barrier, inc=1, device_id=(bulk_at(k), me), device_id_type=MESH)
    for k in range(1, E):
        pl.semaphore_signal(barrier, inc=1, device_id=(mb, expert_at(k)), device_id_type=MESH)
    for k in order:
        weight_copy(0, k).start()
        weight_copy(1, k).start()
    for k in range(B):
        weight_copy(2, k).start()

    slot = lax.broadcasted_iota(jnp.int32, (T, SL), 1)
    slot_expert = lax.div(slot, CAP)
    slot_rank = slot - slot_expert * CAP
    named = jnp.zeros((T, SL), F32)
    gates = jnp.zeros((T, SL), F32)
    member = jnp.zeros((T, E), F32)
    e_iota = lax.broadcasted_iota(jnp.int32, (T, E), 1)
    for j in range(TOP):
        hit = ids[:, j : j + 1] == slot_expert
        named = named + jnp.where(hit, 1.0, 0.0)
        gates = gates + jnp.where(hit, gv[:, j : j + 1], 0.0)
        member = member + jnp.where(ids[:, j : j + 1] == e_iota, 1.0, 0.0)
    t_row = lax.broadcasted_iota(jnp.int32, (T, T), 0)
    t_col = lax.broadcasted_iota(jnp.int32, (T, T), 1)
    below = jnp.where(t_col < t_row, 1.0, 0.0).astype(BF)
    rank = dot(below, named.astype(BF))
    chosen = jnp.where(rank == slot_rank.astype(F32), named, 0.0)
    eye = jnp.where(
        lax.broadcasted_iota(jnp.int32, (SL, SL), 0) == lax.broadcasted_iota(jnp.int32, (SL, SL), 1),
        1.0,
        0.0,
    ).astype(BF)
    selector = lax.dot_general(
        eye, chosen.astype(BF), (((1,), (1,)), ((), ())), preferred_element_type=F32
    ).astype(BF)

    pl.semaphore_wait(barrier, B + E - 2)

    def send1(k):
        return pltpu.make_async_remote_copy(
            og.at[k], oin.at[k], s1.at[k], r1.at[k], device_id=(bulk_at(k), me), device_id_type=MESH
        )

    for k in order:
        cols = pl.ds(pl.multiple_of(bulk_at(k) * DS, 128), DS)
        rows = dot(selector, tok[:, cols]).astype(BF)
        if k:
            og[k] = rows
            send1(k).start()
        else:
            oin[0] = rows

    odd = lax.rem(lax.broadcasted_iota(jnp.int32, (T, E), 0), 2) == 1
    odd_count = jnp.sum(jnp.where(odd, member, 0.0), axis=0, keepdims=True)
    even_count = jnp.sum(jnp.where(odd, 0.0, member), axis=0, keepdims=True)
    er = lax.broadcasted_iota(jnp.int32, (E, E), 0)
    ec = lax.broadcasted_iota(jnp.int32, (E, E), 1)
    shift = jnp.where(lax.rem(er + 1, E) == ec, 1.0, 0.0).astype(BF)
    home = jnp.where(place[...] == ec, 1.0, 0.0).astype(BF)
    spread = lambda count, to: dot(jnp.broadcast_to(count, (8, E)).astype(BF), to)
    load[...] = (spread(odd_count, shift) + spread(even_count, home))[:1].astype(jnp.int32)
    combine = chosen * gates
    c_hi = combine.astype(BF)
    c_rest = combine - c_hi.astype(F32)
    c_mid = c_rest.astype(BF)
    c_lo = (c_rest - c_mid.astype(F32)).astype(BF)

    placed = dot(p1[mb], oin[0])
    for k in range(1, B):
        send1(k).wait_recv()
        placed = placed + dot(p1[bulk_at(-k)], oin[k])
    xs[...] = placed.astype(BF)

    def block(k):
        return pl.ds(pl.multiple_of(k * RP, RP), RP)

    def send2(k):
        return pltpu.make_async_remote_copy(
            xs.at[block(expert_at(k))], xr.at[block(k)], s2.at[k], r2.at[k],
            device_id=(mb, expert_at(k)), device_id_type=MESH,
        )

    for k in range(1, E):
        send2(k).start()
    xr[0:RP] = xs[block(me)]
    for k in range(1, E):
        send2(k).wait_recv()
    x[...] = dot(p2[...], xr[...]).astype(BF)

    def send3(k):
        return pltpu.make_async_remote_copy(
            pout.at[k], pin.at[k], s3.at[k], r3.at[k], device_id=(bulk_at(k), me), device_id_type=MESH
        )

    def partials(k, to):
        weight_copy(0, k).wait()
        weight_copy(1, k).wait()
        to[k, :, :FB] = dot(x[...], wg[k]).astype(BF)
        to[k, :, FB:] = dot(x[...], wu[k]).astype(BF)

    @pl.loop(1, B)
    def _(k):
        partials(k, pout)
        send3(k).start()

    partials(0, pin)
    total = pin[0].astype(F32)
    for k in range(1, B):
        send3(k).wait_recv()
        total = total + pin[k].astype(F32)
    gate = total[:, :FB]
    hin[0] = (gate / (1.0 + jnp.exp(-gate)) * total[:, FB:]).astype(BF)

    def send4(k):
        return pltpu.make_async_remote_copy(
            hin.at[0], hin.at[k], s4.at[k], r4.at[k], device_id=(bulk_at(k), me), device_id_type=MESH
        )

    for k in range(1, B):
        send4(k).start()
    weight_copy(2, 0).wait()
    acc[...] = dot(hin[0], wd[0])

    @pl.loop(1, B)
    def _(k):
        weight_copy(2, k).wait()
        send4(k).wait_recv()
        acc[...] += dot(hin[k], wd[k])

    for k in range(1, E):
        send2(k).wait_send()
    rr = xs
    rr[...] = dot(p2t[...], acc[...].astype(BF)).astype(BF)

    def send5(k):
        return pltpu.make_async_remote_copy(
            rr.at[block(k)], back.at[block(me)], s5.at[k], r5.at[k],
            device_id=(mb, expert_at(-k)), device_id_type=MESH,
        )

    for k in range(1, E):
        send5(k).start()
    back[block(me)] = rr[0:RP]
    for k in range(1, E):
        pltpu.make_async_remote_copy(
            rr.at[block(k)], back.at[block(expert_at(k))], s5.at[k], r5.at[k],
            device_id=(mb, expert_at(-k)), device_id_type=MESH,
        ).wait_recv()

    def send6(k):
        return pltpu.make_async_remote_copy(
            rb.at[k], fin.at[k], s6.at[k], r6.at[k], device_id=(bulk_at(k), me), device_id_type=MESH
        )

    for k in order:
        rows = dot(p1t[bulk_at(k)], back[...]).astype(BF)
        if k:
            rb[k] = rows
            send6(k).start()
        else:
            fin[0] = rows
    for k in range(B):
        if k:
            send6(k).wait_recv()
        rows = fin[k]
        cols = pl.ds(pl.multiple_of(bulk_at(-k) * DS, 128), DS)
        out[:, cols] = (dot(c_hi, rows) + (dot(c_mid, rows) + dot(c_lo, rows))).astype(BF)

    for k in range(1, B):
        send1(k).wait_send()
        send3(k).wait_send()
        send4(k).wait_send()
        send6(k).wait_send()
    for k in range(1, E):
        send5(k).wait_send()


def on_device(tokens, expert_ids, gate_values, placement, gate_weight, up_weight, down_weight):
    E = lax.axis_size("expert")
    B = lax.axis_size("bulk")
    T, D = tokens.shape
    DS = gate_weight.shape[1]
    FB = gate_weight.shape[2] // B
    SL = E * CAP
    RQ = B * CAP
    RP = -(-RQ // 16) * 16
    R = E * RQ
    p1 = np.zeros((B, E * RP, SL), np.float32)
    p2 = np.zeros((R, E * RP), np.float32)
    for e in range(E):
        for q in range(RQ):
            p1[q // CAP, e * RP + q, e * CAP + q % CAP] = 1.0
            p2[e * RQ + q, e * RP + q] = 1.0
    p1t = np.swapaxes(p1, 1, 2)
    consts = [jnp.asarray(a.astype(ml_dtypes.bfloat16)) for a in (p1, p1t, p2, p2.T)]
    vmem = pl.BlockSpec(memory_space=pltpu.VMEM)
    hbm = pl.BlockSpec(memory_space=pl.ANY)
    dma = pltpu.SemaphoreType.DMA
    return pl.pallas_call(
        functools.partial(kernel, B, E, RP),
        out_shape=(
            jax.ShapeDtypeStruct((T, D), BF),
            jax.ShapeDtypeStruct((1, E), jnp.int32),
        ),
        in_specs=[vmem] * 8 + [hbm] * 3,
        out_specs=(vmem, vmem),
        scratch_shapes=[
            pltpu.VMEM((B, DS, FB), BF),
            pltpu.VMEM((B, DS, FB), BF),
            pltpu.VMEM((B, FB, DS), BF),
            pltpu.VMEM((B, SL, DS), BF),
            pltpu.VMEM((B, SL, DS), BF),
            pltpu.VMEM((E * RP, DS), BF),
            pltpu.VMEM((E * RP, DS), BF),
            pltpu.VMEM((R, DS), BF),
            pltpu.VMEM((B, R, 2 * FB), BF),
            pltpu.VMEM((B, R, 2 * FB), BF),
            pltpu.VMEM((B, R, FB), BF),
            pltpu.VMEM((R, DS), F32),
            pltpu.VMEM((E * RP, DS), BF),
            pltpu.VMEM((B, SL, DS), BF),
            pltpu.VMEM((B, SL, DS), BF),
            dma((3, B)),
        ]
        + [dma((n,)) for n in (B, B, E, E, B, B, B, B, E, E, B, B)],
        compiler_params=pltpu.CompilerParams(
            collective_id=0, has_side_effects=True, vmem_limit_bytes=62 * 1024 * 1024
        ),
    )(tokens, expert_ids, gate_values, placement.reshape(E, 1), *consts,
      gate_weight, up_weight, down_weight)


def solution(mesh):
    placed = (
        P(("bulk", "expert"), None),
        P(("bulk", "expert"), None),
        P(("bulk", "expert"), None),
        P(),
        P("expert", "bulk", None),
        P("expert", "bulk", None),
        P("expert", None, "bulk"),
    )
    return jax.shard_map(
        on_device,
        mesh=mesh,
        in_specs=placed,
        out_specs=(P(("bulk", "expert"), None), P(("bulk", "expert"), None)),
        check_vma=False,
    )
```

```python
import functools

import jax
import jax.numpy as jnp
import ml_dtypes
import numpy as np
from jax import lax
from jax.experimental import pallas as pl
from jax.experimental.pallas import tpu as pltpu
from jax.sharding import PartitionSpec as P

CAP = 3
BF = jnp.bfloat16
F32 = jnp.float32
MESH = pl.DeviceIdType.MESH


def dot(a, b):
    return jnp.dot(a, b, preferred_element_type=F32)


def kernel(
    B, E, RP, H, G, tok_hbm, ids, gv, place, p1, p1t, p2, p2t, wg_hbm, wu_hbm, wd_hbm, out, load,
    tok, wg, wu, wd, og, oin, xs, xr, x, pout, pin, hin, acc, back, rb, fin,
    tsem, wsem, s1, r1, s2, r2, s3, r3, s4, r4, s5, r5, s6, r6,
):
    TOP, T = ids.shape
    SL = E * CAP
    DS = wg_hbm.shape[1]
    FB = wg_hbm.shape[2] // B
    DH = DS // H
    FH = FB // G
    mb = lax.axis_index("bulk")
    me = lax.axis_index("expert")

    def bulk_at(k):
        return lax.rem(mb + k + B, B)

    def expert_at(k):
        return lax.rem(me + k + E, E)

    def weight_copy(i, k):
        if i == 2:
            rows = pl.ds(pl.multiple_of(bulk_at(-k) * FB, FB), FB)
            return pltpu.make_async_copy(wd_hbm.at[0, rows, :], wd.at[k], wsem.at[2, k])
        cols = pl.ds(pl.multiple_of(bulk_at(k) * FB, FB), FB)
        source, to = ((wg_hbm, wg), (wu_hbm, wu))[i]
        return pltpu.make_async_copy(source.at[0, :, cols], to.at[k], wsem.at[i, k])

    tok_copy = pltpu.make_async_copy(tok_hbm, tok, tsem)
    tok_copy.start()
    far_first = [(i + B // 2 - 1) % (B - 1) + 1 for i in range(B - 1)]
    order = far_first + [0]
    barrier = pltpu.get_barrier_semaphore()
    for k in range(1, B):
        pl.semaphore_signal(barrier, inc=1, device_id=(bulk_at(k), me), device_id_type=MESH)
    for k in range(1, E):
        pl.semaphore_signal(barrier, inc=1, device_id=(mb, expert_at(k)), device_id_type=MESH)

    slot = lax.broadcasted_iota(jnp.int32, (SL, T), 0)
    slot_expert = lax.div(slot, CAP)
    slot_rank = slot - slot_expert * CAP
    named = jnp.zeros((SL, T), F32)
    gates = jnp.zeros((SL, T), F32)
    for j in range(TOP):
        hit = ids[j : j + 1, :] == slot_expert
        named = named + jnp.where(hit, 1.0, 0.0)
        gates = gates + jnp.where(hit, gv[j : j + 1, :], 0.0)
    t_row = lax.broadcasted_iota(jnp.int32, (T, T), 0)
    t_col = lax.broadcasted_iota(jnp.int32, (T, T), 1)
    before = jnp.where(t_row < t_col, 1.0, 0.0).astype(BF)
    rank = dot(named.astype(BF), before)
    chosen = jnp.where(rank == slot_rank.astype(F32), named, 0.0)
    selector = chosen.astype(BF)

    def send1(k, h):
        return pltpu.make_async_remote_copy(
            og.at[k, h], oin.at[k, h], s1.at[k, h], r1.at[k, h],
            device_id=(bulk_at(k), me), device_id_type=MESH,
        )

    pl.semaphore_wait(barrier, B + E - 2)
    tok_copy.wait()
    for h in range(H):
        for k in order:
            cols = pl.ds(pl.multiple_of(bulk_at(k) * DS + h * DH, 128), DH)
            rows = dot(selector, tok[:, cols]).astype(BF)
            if k:
                og[k, h] = rows
                send1(k, h).start()
            else:
                oin[0, h] = rows
    for k in order:
        weight_copy(0, k).start()
        weight_copy(1, k).start()
    for k in range(B):
        weight_copy(2, k).start()

    member = jnp.zeros((E, T), F32)
    e_iota = lax.broadcasted_iota(jnp.int32, (E, T), 0)
    for j in range(TOP):
        member = member + jnp.where(ids[j : j + 1, :] == e_iota, 1.0, 0.0)
    odd_t = lax.rem(lax.broadcasted_iota(jnp.int32, (8, T), 1), 2) == 1
    odd = jnp.where(odd_t, 1.0, 0.0).astype(BF)
    even = jnp.where(odd_t, 0.0, 1.0).astype(BF)
    er = lax.broadcasted_iota(jnp.int32, (E, E), 0)
    ec = lax.broadcasted_iota(jnp.int32, (E, E), 1)
    shift = jnp.where(er == lax.rem(ec + 1, E), 1.0, 0.0).astype(BF)
    home = jnp.where(er == place[...], 1.0, 0.0).astype(BF)

    def across(a, b):
        return lax.dot_general(a, b, (((1,), (1,)), ((), ())), preferred_element_type=F32)

    member = member.astype(BF)
    loads = across(across(odd, member).astype(BF), shift) + across(
        across(even, member).astype(BF), home
    )
    load[...] = loads[:1].astype(jnp.int32)
    eye = jnp.where(t_row == t_col, 1.0, 0.0).astype(BF)
    combine = chosen * gates
    c_hi = combine.astype(BF)
    c_rest = combine - c_hi.astype(F32)
    c_mid = c_rest.astype(BF)
    c_lo = (c_rest - c_mid.astype(F32)).astype(BF)
    c_hi, c_mid, c_lo = (across(eye, c).astype(BF) for c in (c_hi, c_mid, c_lo))

    def block(k):
        return pl.ds(pl.multiple_of(k * RP, RP), RP)

    def send2(k, h):
        return pltpu.make_async_remote_copy(
            xs.at[h, block(expert_at(k))], xr.at[h, block(k)], s2.at[k, h], r2.at[k, h],
            device_id=(mb, expert_at(k)), device_id_type=MESH,
        )

    for h in range(H):
        rows = dot(p1[mb], oin[0, h])
        for k in range(1, B):
            send1(k, h).wait_recv()
            rows = rows + dot(p1[bulk_at(-k)], oin[k, h])
        xs[h] = rows.astype(BF)
        for k in range(1, E):
            send2(k, h).start()
        xr[h, 0:RP] = xs[h, block(me)]
    for h in range(H):
        for k in range(1, E):
            send2(k, h).wait_recv()
        x[:, h * DH : (h + 1) * DH] = dot(p2[...], xr[h]).astype(BF)

    def send3(k, q):
        return pltpu.make_async_remote_copy(
            pout.at[q, k], pin.at[q, k], s3.at[k, q], r3.at[k, q],
            device_id=(bulk_at(k), me), device_id_type=MESH,
        )

    def partials(k, q, to):
        cols = slice(q * FH, (q + 1) * FH)
        to[q, k, :, :FH] = dot(x[...], wg[k, :, cols]).astype(BF)
        to[q, k, :, FH:] = dot(x[...], wu[k, :, cols]).astype(BF)

    for q in range(G):

        @pl.loop(0, B - 1)
        def _(i):
            k = lax.rem(i + (B // 2 - 1), B - 1) + 1
            if q == 0:
                weight_copy(0, k).wait()
                weight_copy(1, k).wait()
            partials(k, q, pout)
            send3(k, q).start()

    weight_copy(0, 0).wait()
    weight_copy(1, 0).wait()

    def send4(k, q):
        return pltpu.make_async_remote_copy(
            hin.at[q, 0], hin.at[q, k], s4.at[k, q], r4.at[k, q],
            device_id=(bulk_at(k), me), device_id_type=MESH,
        )

    for q in range(G):
        partials(0, q, pin)
    for q in range(G):
        total = pin[q, 0].astype(F32)
        for k in range(1, B):
            send3(k, q).wait_recv()
            total = total + pin[q, k].astype(F32)
        gate = total[:, :FH]
        hin[q, 0] = (gate / (1.0 + jnp.exp(-gate)) * total[:, FH:]).astype(BF)
        for k in far_first:
            send4(k, q).start()
    weight_copy(2, 0).wait()
    acc[...] = dot(hin[0, 0], wd[0, 0:FH])
    for q in range(1, G):
        acc[...] += dot(hin[q, 0], wd[0, q * FH : (q + 1) * FH])
    for k in range(1, B):
        weight_copy(2, k).wait()
    for q in range(G):

        @pl.loop(1, B - 1 if q == G - 1 else B)
        def _(k):
            send4(k, q).wait_recv()
            acc[...] += dot(hin[q, k], wd[k, q * FH : (q + 1) * FH])

    rr = xs

    def send5(k, h, at):
        return pltpu.make_async_remote_copy(
            rr.at[h, block(k)], back.at[h, block(at)], s5.at[k, h], r5.at[k, h],
            device_id=(mb, expert_at(-k)), device_id_type=MESH,
        )

    send4(B - 1, G - 1).wait_recv()
    for h in range(H):
        for k in range(1, E):
            send2(k, h).wait_send()
        cols = slice(h * DH, (h + 1) * DH)
        rows = acc[:, cols] + dot(hin[G - 1, B - 1], wd[B - 1, (G - 1) * FH : G * FH, cols])
        rr[h] = dot(p2t[...], rows.astype(BF)).astype(BF)
        for k in range(1, E):
            send5(k, h, me).start()
        back[h, block(me)] = rr[h, 0:RP]

    def send6(k, h):
        return pltpu.make_async_remote_copy(
            rb.at[k, h], fin.at[k, h], s6.at[k, h], r6.at[k, h],
            device_id=(bulk_at(k), me), device_id_type=MESH,
        )

    for h in range(H):
        for k in range(1, E):
            send5(k, h, expert_at(k)).wait_recv()
        for k in order:
            rows = dot(p1t[bulk_at(k)], back[h]).astype(BF)
            if k:
                rb[k, h] = rows
                send6(k, h).start()
            else:
                fin[0, h] = rows
    for h in range(H):
        for k in range(B):
            if k:
                send6(k, h).wait_recv()
            rows = fin[k, h]
            cols = pl.ds(pl.multiple_of(bulk_at(-k) * DS + h * DH, 128), DH)
            out[:, cols] = (dot(c_hi, rows) + (dot(c_mid, rows) + dot(c_lo, rows))).astype(BF)

    for k in range(1, B):
        for h in range(H):
            send1(k, h).wait_send()
            send6(k, h).wait_send()
        for q in range(G):
            send3(k, q).wait_send()
            send4(k, q).wait_send()
    for k in range(1, E):
        for h in range(H):
            send5(k, h, me).wait_send()


def on_device(tokens, expert_ids, gate_values, placement, gate_weight, up_weight, down_weight):
    E = lax.axis_size("expert")
    B = lax.axis_size("bulk")
    T, D = tokens.shape
    DS = gate_weight.shape[1]
    FB = gate_weight.shape[2] // B
    SL = E * CAP
    RQ = B * CAP
    RP = -(-RQ // 16) * 16
    R = E * RQ
    p1 = np.zeros((B, E * RP, SL), np.float32)
    p2 = np.zeros((R, E * RP), np.float32)
    for e in range(E):
        for q in range(RQ):
            p1[q // CAP, e * RP + q, e * CAP + q % CAP] = 1.0
            p2[e * RQ + q, e * RP + q] = 1.0
    p1t = np.swapaxes(p1, 1, 2)
    consts = [jnp.asarray(a.astype(ml_dtypes.bfloat16)) for a in (p1, p1t, p2, p2.T)]
    H = 2 if DS % 256 == 0 else 1
    G = 2 if FB % 256 == 0 else 1
    DH = DS // H
    FH = FB // G
    vmem = pl.BlockSpec(memory_space=pltpu.VMEM)
    hbm = pl.BlockSpec(memory_space=pl.ANY)
    dma = pltpu.SemaphoreType.DMA
    buffers = [
        (T, D), (B, DS, FB), (B, DS, FB), (B, FB, DS),
        (B, H, SL, DH), (B, H, SL, DH), (H, E * RP, DH), (H, E * RP, DH), (R, DS),
        (G, B, R, 2 * FH), (G, B, R, 2 * FH), (G, B, R, FH), (R, DS),
        (H, E * RP, DH), (B, H, SL, DH), (B, H, SL, DH),
    ]
    sems = [(B, H), (B, H), (E, H), (E, H)] + [(B, G)] * 4 + [(E, H), (E, H), (B, H), (B, H)]
    return pl.pallas_call(
        functools.partial(kernel, B, E, RP, H, G),
        out_shape=(
            jax.ShapeDtypeStruct((T, D), BF),
            jax.ShapeDtypeStruct((1, E), jnp.int32),
        ),
        in_specs=[hbm] + [vmem] * 7 + [hbm] * 3,
        out_specs=(vmem, vmem),
        scratch_shapes=[pltpu.VMEM(d, F32 if i == 12 else BF) for i, d in enumerate(buffers)]
        + [dma, dma((3, B))]
        + [dma(n) for n in sems],
        compiler_params=pltpu.CompilerParams(
            collective_id=0, has_side_effects=True, vmem_limit_bytes=62 * 1024 * 1024
        ),
    )(tokens, expert_ids.T, gate_values.T, placement.reshape(1, E), *consts,
      gate_weight, up_weight, down_weight)


def solution(mesh):
    placed = (
        P(("bulk", "expert"), None),
        P(("bulk", "expert"), None),
        P(("bulk", "expert"), None),
        P(),
        P("expert", "bulk", None),
        P("expert", "bulk", None),
        P("expert", None, "bulk"),
    )
    return jax.shard_map(
        on_device,
        mesh=mesh,
        in_specs=placed,
        out_specs=(P(("bulk", "expert"), None), P(("bulk", "expert"), None)),
        check_vma=False,
    )
```

```python
import functools

import jax
import jax.numpy as jnp
import ml_dtypes
import numpy as np
from jax import lax
from jax.experimental import pallas as pl
from jax.experimental.pallas import tpu as pltpu
from jax.sharding import PartitionSpec as P

CAP = 3
BF = jnp.bfloat16
F32 = jnp.float32
MESH = pl.DeviceIdType.MESH


def dot(a, b):
    return jnp.dot(a, b, preferred_element_type=F32)


def kernel(
    B, E, RP, H, G, tok_hbm, ids, gv, place, p1, p1t, p2, p2t, wg_hbm, wu_hbm, wd_hbm,
    fin, cs, ld, tok, wg, wu, wd, og, oin, xs, xr, x, pout, pin, hin, acc, back, rb, csv, ldv,
    tsem, csem, fsem, wsem, s1, r1, s2, r2, s3, r3, s4, r4, s5, r5, s6, r6,
):
    TOP, T = ids.shape
    SL = E * CAP
    DS = wg_hbm.shape[1]
    FB = wg_hbm.shape[2] // B
    DH = DS // H
    FH = FB // G
    mb = lax.axis_index("bulk")
    me = lax.axis_index("expert")

    def bulk_at(k):
        return lax.rem(mb + k + B, B)

    def expert_at(k):
        return lax.rem(me + k + E, E)

    def weight_copy(i, k):
        if i == 2:
            rows = pl.ds(pl.multiple_of(bulk_at(-k) * FB, FB), FB)
            return pltpu.make_async_copy(wd_hbm.at[0, rows, :], wd.at[k], wsem.at[2, k])
        cols = pl.ds(pl.multiple_of(bulk_at(k) * FB, FB), FB)
        source, to = ((wg_hbm, wg), (wu_hbm, wu))[i]
        return pltpu.make_async_copy(source.at[0, :, cols], to.at[k], wsem.at[i, k])

    tok_copy = pltpu.make_async_copy(tok_hbm, tok, tsem)
    tok_copy.start()
    far_first = [(i + B // 2 - 1) % (B - 1) + 1 for i in range(B - 1)]
    order = far_first + [0]
    barrier = pltpu.get_barrier_semaphore()
    for k in range(1, B):
        pl.semaphore_signal(barrier, inc=1, device_id=(bulk_at(k), me), device_id_type=MESH)
    for k in range(1, E):
        pl.semaphore_signal(barrier, inc=1, device_id=(mb, expert_at(k)), device_id_type=MESH)

    slot = lax.broadcasted_iota(jnp.int32, (SL, T), 0)
    slot_expert = lax.div(slot, CAP)
    slot_rank = slot - slot_expert * CAP
    named = jnp.zeros((SL, T), F32)
    gates = jnp.zeros((SL, T), F32)
    for j in range(TOP):
        hit = ids[j : j + 1, :] == slot_expert
        named = named + jnp.where(hit, 1.0, 0.0)
        gates = gates + jnp.where(hit, gv[j : j + 1, :], 0.0)
    t_row = lax.broadcasted_iota(jnp.int32, (T, T), 0)
    t_col = lax.broadcasted_iota(jnp.int32, (T, T), 1)
    before = jnp.where(t_row < t_col, 1.0, 0.0).astype(BF)
    rank = dot(named.astype(BF), before)
    chosen = jnp.where(rank == slot_rank.astype(F32), named, 0.0)
    selector = chosen.astype(BF)

    def send1(k, h):
        return pltpu.make_async_remote_copy(
            og.at[k, h], oin.at[k, h], s1.at[k, h], r1.at[k, h],
            device_id=(bulk_at(k), me), device_id_type=MESH,
        )

    pl.semaphore_wait(barrier, B + E - 2)
    tok_copy.wait()
    for h in range(H):
        for k in order:
            cols = pl.ds(pl.multiple_of(bulk_at(k) * DS + h * DH, 128), DH)
            rows = dot(selector, tok[:, cols]).astype(BF)
            if k:
                og[k, h] = rows
                send1(k, h).start()
            else:
                oin[0, h] = rows
    for k in order:
        weight_copy(0, k).start()
        weight_copy(1, k).start()
    for k in range(B):
        weight_copy(2, k).start()

    member = jnp.zeros((E, T), F32)
    e_iota = lax.broadcasted_iota(jnp.int32, (E, T), 0)
    for j in range(TOP):
        member = member + jnp.where(ids[j : j + 1, :] == e_iota, 1.0, 0.0)
    odd_t = lax.rem(lax.broadcasted_iota(jnp.int32, (8, T), 1), 2) == 1
    odd = jnp.where(odd_t, 1.0, 0.0).astype(BF)
    even = jnp.where(odd_t, 0.0, 1.0).astype(BF)
    er = lax.broadcasted_iota(jnp.int32, (E, E), 0)
    ec = lax.broadcasted_iota(jnp.int32, (E, E), 1)
    shift = jnp.where(er == lax.rem(ec + 1, E), 1.0, 0.0).astype(BF)
    home = jnp.where(er == place[...], 1.0, 0.0).astype(BF)

    def across(a, b):
        return lax.dot_general(a, b, (((1,), (1,)), ((), ())), preferred_element_type=F32)

    member = member.astype(BF)
    loads = across(across(odd, member).astype(BF), shift) + across(
        across(even, member).astype(BF), home
    )
    ldv[...] = loads
    eye = jnp.where(t_row == t_col, 1.0, 0.0).astype(BF)
    combine = chosen * gates
    c_hi = combine.astype(BF)
    c_rest = combine - c_hi.astype(F32)
    c_mid = c_rest.astype(BF)
    c_lo = (c_rest - c_mid.astype(F32)).astype(BF)
    for i, c in enumerate((c_hi, c_mid, c_lo)):
        csv[i] = across(eye, c).astype(BF)
    side = (
        pltpu.make_async_copy(csv, cs, csem.at[0]),
        pltpu.make_async_copy(ldv, ld, csem.at[1]),
    )
    for copy in side:
        copy.start()

    def block(k):
        return pl.ds(pl.multiple_of(k * RP, RP), RP)

    def send2(k, h):
        return pltpu.make_async_remote_copy(
            xs.at[h, block(expert_at(k))], xr.at[h, block(k)], s2.at[k, h], r2.at[k, h],
            device_id=(mb, expert_at(k)), device_id_type=MESH,
        )

    for h in range(H):
        rows = dot(p1[mb], oin[0, h])
        for k in range(1, B):
            send1(k, h).wait_recv()
            rows = rows + dot(p1[bulk_at(-k)], oin[k, h])
        xs[h] = rows.astype(BF)
        for k in range(1, E):
            send2(k, h).start()
        xr[h, 0:RP] = xs[h, block(me)]
    for h in range(H):
        for k in range(1, E):
            send2(k, h).wait_recv()
        x[:, h * DH : (h + 1) * DH] = dot(p2[...], xr[h]).astype(BF)

    def send3(k, q):
        return pltpu.make_async_remote_copy(
            pout.at[q, k], pin.at[q, k], s3.at[k, q], r3.at[k, q],
            device_id=(bulk_at(k), me), device_id_type=MESH,
        )

    def partials(k, q, to):
        cols = slice(q * FH, (q + 1) * FH)
        to[q, k, :, :FH] = dot(x[...], wg[k, :, cols]).astype(BF)
        to[q, k, :, FH:] = dot(x[...], wu[k, :, cols]).astype(BF)

    for q in range(G):

        @pl.loop(0, B - 1)
        def _(i):
            k = lax.rem(i + (B // 2 - 1), B - 1) + 1
            if q == 0:
                weight_copy(0, k).wait()
                weight_copy(1, k).wait()
            partials(k, q, pout)
            send3(k, q).start()

    weight_copy(0, 0).wait()
    weight_copy(1, 0).wait()

    def send4(k, q):
        return pltpu.make_async_remote_copy(
            hin.at[q, 0], hin.at[q, k], s4.at[k, q], r4.at[k, q],
            device_id=(bulk_at(k), me), device_id_type=MESH,
        )

    for q in range(G):
        partials(0, q, pin)
    for q in range(G):
        total = pin[q, 0].astype(F32)
        for k in range(1, B):
            send3(k, q).wait_recv()
            total = total + pin[q, k].astype(F32)
        gate = total[:, :FH]
        hin[q, 0] = (gate / (1.0 + jnp.exp(-gate)) * total[:, FH:]).astype(BF)
        for k in far_first:
            send4(k, q).start()
    weight_copy(2, 0).wait()
    acc[...] = dot(hin[0, 0], wd[0, 0:FH])
    for q in range(1, G):
        acc[...] += dot(hin[q, 0], wd[0, q * FH : (q + 1) * FH])
    for k in range(1, B):
        weight_copy(2, k).wait()
    for q in range(G):

        @pl.loop(1, B - 1 if q == G - 1 else B)
        def _(k):
            send4(k, q).wait_recv()
            acc[...] += dot(hin[q, k], wd[k, q * FH : (q + 1) * FH])

    rr = xs

    def send5(k, h, at):
        return pltpu.make_async_remote_copy(
            rr.at[h, block(k)], back.at[h, block(at)], s5.at[k, h], r5.at[k, h],
            device_id=(mb, expert_at(-k)), device_id_type=MESH,
        )

    send4(B - 1, G - 1).wait_recv()
    for h in range(H):
        for k in range(1, E):
            send2(k, h).wait_send()
        cols = slice(h * DH, (h + 1) * DH)
        rows = acc[:, cols] + dot(hin[G - 1, B - 1], wd[B - 1, (G - 1) * FH : G * FH, cols])
        rr[h] = dot(p2t[...], rows.astype(BF)).astype(BF)
        for k in range(1, E):
            send5(k, h, me).start()
        back[h, block(me)] = rr[h, 0:RP]

    def send6(k, h, at):
        return pltpu.make_async_remote_copy(
            rb.at[k, h], fin.at[at, h], s6.at[k, h], r6.at[k, h],
            device_id=(bulk_at(k), me), device_id_type=MESH,
        )

    def keep(h):
        return pltpu.make_async_copy(rb.at[0, h], fin.at[mb, h], fsem.at[h])

    for h in range(H):
        for k in range(1, E):
            send5(k, h, expert_at(k)).wait_recv()
        for k in order:
            rb[k, h] = dot(p1t[bulk_at(k)], back[h]).astype(BF)
            if k:
                send6(k, h, mb).start()
            else:
                keep(h).start()
    for copy in side:
        copy.wait()
    for k in range(1, B):
        for h in range(H):
            send1(k, h).wait_send()
            send6(k, h, mb).wait_send()
        for q in range(G):
            send3(k, q).wait_send()
            send4(k, q).wait_send()
    for k in range(1, E):
        for h in range(H):
            send5(k, h, me).wait_send()
    for h in range(H):
        keep(h).wait()
        for k in range(1, B):
            send6(k, h, bulk_at(-k)).wait_recv()


def combine_kernel(fin, cs, ld, out_hbm, load, out, sems):
    B, H, SL, DH = fin.shape
    load[...] = ld[:1].astype(jnp.int32)
    copies = []
    for b in range(B):
        for h in range(H):
            rows = fin[b, h]
            at = (b * H + h) * DH
            out[:, at : at + DH] = (
                dot(cs[0], rows) + (dot(cs[1], rows) + dot(cs[2], rows))
            ).astype(BF)
        cols = pl.ds(b * H * DH, H * DH)
        copies.append(pltpu.make_async_copy(out.at[:, cols], out_hbm.at[:, cols], sems.at[b]))
        copies[-1].start()
    for copy in copies:
        copy.wait()


def on_device(tokens, expert_ids, gate_values, placement, gate_weight, up_weight, down_weight):
    E = lax.axis_size("expert")
    B = lax.axis_size("bulk")
    T, D = tokens.shape
    DS = gate_weight.shape[1]
    FB = gate_weight.shape[2] // B
    SL = E * CAP
    RQ = B * CAP
    RP = -(-RQ // 16) * 16
    R = E * RQ
    p1 = np.zeros((B, E * RP, SL), np.float32)
    p2 = np.zeros((R, E * RP), np.float32)
    for e in range(E):
        for q in range(RQ):
            p1[q // CAP, e * RP + q, e * CAP + q % CAP] = 1.0
            p2[e * RQ + q, e * RP + q] = 1.0
    p1t = np.swapaxes(p1, 1, 2)
    consts = [jnp.asarray(a.astype(ml_dtypes.bfloat16)) for a in (p1, p1t, p2, p2.T)]
    H = 2 if DS % 256 == 0 else 1
    G = 2 if FB % 256 == 0 else 1
    DH = DS // H
    FH = FB // G
    vmem = pl.BlockSpec(memory_space=pltpu.VMEM)
    hbm = pl.BlockSpec(memory_space=pl.ANY)
    dma = pltpu.SemaphoreType.DMA
    buffers = [
        (T, D), (B, DS, FB), (B, DS, FB), (B, FB, DS),
        (B, H, SL, DH), (B, H, SL, DH), (H, E * RP, DH), (H, E * RP, DH), (R, DS),
        (G, B, R, 2 * FH), (G, B, R, 2 * FH), (G, B, R, FH), (R, DS),
        (H, E * RP, DH), (B, H, SL, DH), (3, T, SL), (8, E),
    ]
    sems = [(B, H), (B, H), (E, H), (E, H)] + [(B, G)] * 4 + [(E, H), (E, H), (B, H), (B, H)]
    fin, cs, ld = pl.pallas_call(
        functools.partial(kernel, B, E, RP, H, G),
        out_shape=(
            jax.ShapeDtypeStruct((B, H, SL, DH), BF),
            jax.ShapeDtypeStruct((3, T, SL), BF),
            jax.ShapeDtypeStruct((8, E), F32),
        ),
        in_specs=[hbm] + [vmem] * 7 + [hbm] * 3,
        out_specs=(hbm, hbm, hbm),
        scratch_shapes=[pltpu.VMEM(d, F32 if i in (12, 16) else BF) for i, d in enumerate(buffers)]
        + [dma, dma((2,)), dma((H,)), dma((3, B))]
        + [dma(n) for n in sems],
        compiler_params=pltpu.CompilerParams(
            collective_id=0, has_side_effects=True, vmem_limit_bytes=62 * 1024 * 1024
        ),
    )(tokens, expert_ids.T, gate_values.T, placement.reshape(1, E), *consts,
      gate_weight, up_weight, down_weight)
    return pl.pallas_call(
        combine_kernel,
        out_shape=(
            jax.ShapeDtypeStruct((T, D), BF),
            jax.ShapeDtypeStruct((1, E), jnp.int32),
        ),
        in_specs=[vmem] * 3,
        out_specs=(hbm, vmem),
        scratch_shapes=[pltpu.VMEM((T, D), BF), dma((B,))],
    )(fin, cs, ld)


def solution(mesh):
    placed = (
        P(("bulk", "expert"), None),
        P(("bulk", "expert"), None),
        P(("bulk", "expert"), None),
        P(),
        P("expert", "bulk", None),
        P("expert", "bulk", None),
        P("expert", None, "bulk"),
    )
    return jax.shard_map(
        on_device,
        mesh=mesh,
        in_specs=placed,
        out_specs=(P(("bulk", "expert"), None), P(("bulk", "expert"), None)),
        check_vma=False,
    )
```

```python
import functools

import jax
import jax.numpy as jnp
import ml_dtypes
import numpy as np
from jax import lax
from jax.experimental import pallas as pl
from jax.experimental.pallas import tpu as pltpu
from jax.sharding import PartitionSpec as P

CAP = 3
BF = jnp.bfloat16
F32 = jnp.float32
MESH = pl.DeviceIdType.MESH


def dot(a, b):
    return jnp.dot(a, b, preferred_element_type=F32)


def kernel(
    B, E, RP, H, G, tok_hbm, ids, gv, place, p1, p1t, p2, p2t, wg_hbm, wu_hbm, wd_hbm,
    fin, cs, ld, tok, wg, wu, wd, og, oin, xs, xr, x, pout, pin, hin, acc, back, rb, csv, ldv,
    tsem, csem, fsem, wsem, s1, r1, s2, r2, s3, r3, s4, r4, s5, r5, s6, r6,
):
    TOP, T = ids.shape
    SL = E * CAP
    DS = wg_hbm.shape[1]
    FB = wg_hbm.shape[2] // B
    DH = DS // H
    FH = FB // G
    mb = lax.axis_index("bulk")
    me = lax.axis_index("expert")

    def bulk_at(k):
        return lax.rem(mb + k + B, B)

    def expert_at(k):
        return lax.rem(me + k + E, E)

    def weight_copy(i, k):
        if i == 2:
            rows = pl.ds(pl.multiple_of(bulk_at(-k) * FB, FB), FB)
            return pltpu.make_async_copy(wd_hbm.at[0, rows, :], wd.at[k], wsem.at[2, k])
        cols = pl.ds(pl.multiple_of(bulk_at(k) * FB, FB), FB)
        source, to = ((wg_hbm, wg), (wu_hbm, wu))[i]
        return pltpu.make_async_copy(source.at[0, :, cols], to.at[k], wsem.at[i, k])

    tok_copy = pltpu.make_async_copy(tok_hbm, tok, tsem)
    tok_copy.start()
    far_first = [(i + B // 2 - 1) % (B - 1) + 1 for i in range(B - 1)]
    order = far_first + [0]
    barrier = pltpu.get_barrier_semaphore()
    for k in range(1, B):
        pl.semaphore_signal(barrier, inc=1, device_id=(bulk_at(k), me), device_id_type=MESH)
    for k in range(1, E):
        pl.semaphore_signal(barrier, inc=1, device_id=(mb, expert_at(k)), device_id_type=MESH)

    slot = lax.broadcasted_iota(jnp.int32, (SL, T), 0)
    slot_expert = lax.div(slot, CAP)
    slot_rank = slot - slot_expert * CAP
    named = jnp.zeros((SL, T), F32)
    gates = jnp.zeros((SL, T), F32)
    for j in range(TOP):
        hit = ids[j : j + 1, :] == slot_expert
        named = named + jnp.where(hit, 1.0, 0.0)
        gates = gates + jnp.where(hit, gv[j : j + 1, :], 0.0)
    t_row = lax.broadcasted_iota(jnp.int32, (T, T), 0)
    t_col = lax.broadcasted_iota(jnp.int32, (T, T), 1)
    before = jnp.where(t_row < t_col, 1.0, 0.0).astype(BF)
    rank = dot(named.astype(BF), before)
    chosen = jnp.where(rank == slot_rank.astype(F32), named, 0.0)
    selector = chosen.astype(BF)

    def send1(k, h):
        return pltpu.make_async_remote_copy(
            og.at[k, h], oin.at[k, h], s1.at[k, h], r1.at[k, h],
            device_id=(bulk_at(k), me), device_id_type=MESH,
        )

    pl.semaphore_wait(barrier, B + E - 2)
    tok_copy.wait()
    for h in range(H):
        for k in order:
            cols = pl.ds(pl.multiple_of(bulk_at(k) * DS + h * DH, 128), DH)
            rows = dot(selector, tok[:, cols]).astype(BF)
            if k:
                og[k, h] = rows
                send1(k, h).start()
            else:
                oin[0, h] = rows
    for k in order:
        weight_copy(0, k).start()
        weight_copy(1, k).start()
    for k in range(B):
        weight_copy(2, k).start()

    member = jnp.zeros((E, T), F32)
    e_iota = lax.broadcasted_iota(jnp.int32, (E, T), 0)
    for j in range(TOP):
        member = member + jnp.where(ids[j : j + 1, :] == e_iota, 1.0, 0.0)
    odd_t = lax.rem(lax.broadcasted_iota(jnp.int32, (8, T), 1), 2) == 1
    odd = jnp.where(odd_t, 1.0, 0.0).astype(BF)
    even = jnp.where(odd_t, 0.0, 1.0).astype(BF)
    er = lax.broadcasted_iota(jnp.int32, (E, E), 0)
    ec = lax.broadcasted_iota(jnp.int32, (E, E), 1)
    shift = jnp.where(er == lax.rem(ec + 1, E), 1.0, 0.0).astype(BF)
    home = jnp.where(er == place[...], 1.0, 0.0).astype(BF)

    def across(a, b):
        return lax.dot_general(a, b, (((1,), (1,)), ((), ())), preferred_element_type=F32)

    member = member.astype(BF)
    loads = across(across(odd, member).astype(BF), shift) + across(
        across(even, member).astype(BF), home
    )
    ldv[...] = loads
    eye = jnp.where(t_row == t_col, 1.0, 0.0).astype(BF)
    combine = chosen * gates
    c_hi = combine.astype(BF)
    c_rest = combine - c_hi.astype(F32)
    c_mid = c_rest.astype(BF)
    c_lo = (c_rest - c_mid.astype(F32)).astype(BF)
    for i, c in enumerate((c_hi, c_mid, c_lo)):
        csv[i] = across(eye, c).astype(BF)
    side = (
        pltpu.make_async_copy(csv, cs, csem.at[0]),
        pltpu.make_async_copy(ldv, ld, csem.at[1]),
    )
    for copy in side:
        copy.start()

    def block(k):
        return pl.ds(pl.multiple_of(k * RP, RP), RP)

    def send2(k, h):
        return pltpu.make_async_remote_copy(
            xs.at[h, block(expert_at(k))], xr.at[h, block(k)], s2.at[k, h], r2.at[k, h],
            device_id=(mb, expert_at(k)), device_id_type=MESH,
        )

    for h in range(H):
        rows = dot(p1[mb], oin[0, h])
        for k in range(1, B):
            send1(k, h).wait_recv()
            rows = rows + dot(p1[bulk_at(-k)], oin[k, h])
        xs[h] = rows.astype(BF)
        for k in range(1, E):
            send2(k, h).start()
        xr[h, 0:RP] = xs[h, block(me)]
    for h in range(H):
        for k in range(1, E):
            send2(k, h).wait_recv()
        x[:, h * DH : (h + 1) * DH] = dot(p2[...], xr[h]).astype(BF)

    pair = lax.div(mb, 2)
    is_odd = lax.rem(mb, 2)
    partner = mb + 1 - 2 * is_odd

    def direct(d, q):
        return pltpu.make_async_remote_copy(
            pout.at[q, d], pin.at[q, pair], s3.at[d, q], r3.at[pair, q],
            device_id=(d, me), device_id_type=MESH,
        )

    def relay(d, q):
        return pltpu.make_async_remote_copy(
            pout.at[q, d], pin.at[q, B // 2 + d], s3.at[d, q], r3.at[B // 2 + d, q],
            device_id=(partner, me), device_id_type=MESH,
        )

    def arrival(p, q):
        return pltpu.make_async_remote_copy(
            pout.at[q, mb], pin.at[q, p], s3.at[mb, q], r3.at[p, q],
            device_id=(partner, me), device_id_type=MESH,
        )

    def above(d):
        return jnp.where(lax.div(d, 2) > pair, 1, 0)

    def partials(d, k, q):
        cols = slice(q * FH, (q + 1) * FH)
        pout[q, d, :, :FH] = dot(x[...], wg[k, :, cols]).astype(BF)
        pout[q, d, :, FH:] = dot(x[...], wu[k, :, cols]).astype(BF)

    for q in range(G):

        @pl.loop(0, B - 1)
        def _(i):
            k = lax.rem(i + (B // 2 - 1), B - 1) + 1
            d = bulk_at(k)
            if q == 0:
                weight_copy(0, k).wait()
                weight_copy(1, k).wait()
            partials(d, k, q)

            @pl.when(d == partner)
            def _():
                direct(d, q).start()

            @pl.when((d != partner) & (above(d) != is_odd))
            def _():
                relay(d, q).start()

    weight_copy(0, 0).wait()
    weight_copy(1, 0).wait()
    for q in range(G):
        partials(mb, 0, q)

    for q in range(G):

        @pl.loop(0, B - 1)
        def _(i):
            d = bulk_at(lax.rem(i + (B // 2 - 1), B - 1) + 1)

            @pl.when((d != partner) & (above(d) == is_odd))
            def _():
                arrival(B // 2 + d, q).wait_recv()
                both = pout[q, d].astype(F32) + pin[q, B // 2 + d].astype(F32)
                pout[q, d] = both.astype(BF)
                direct(d, q).start()

    def send4(k, q):
        return pltpu.make_async_remote_copy(
            hin.at[q, 0], hin.at[q, k], s4.at[k, q], r4.at[k, q],
            device_id=(bulk_at(k), me), device_id_type=MESH,
        )

    for q in range(G):
        total = pout[q, mb].astype(F32)
        for p in range(B // 2):
            arrival(p, q).wait_recv()
            total = total + pin[q, p].astype(F32)
        gate = total[:, :FH]
        hin[q, 0] = (gate / (1.0 + jnp.exp(-gate)) * total[:, FH:]).astype(BF)
        for k in far_first:
            send4(k, q).start()
    weight_copy(2, 0).wait()
    acc[...] = dot(hin[0, 0], wd[0, 0:FH])
    for q in range(1, G):
        acc[...] += dot(hin[q, 0], wd[0, q * FH : (q + 1) * FH])
    for k in range(1, B):
        weight_copy(2, k).wait()
    for q in range(G):

        @pl.loop(1, B - 1 if q == G - 1 else B)
        def _(k):
            send4(k, q).wait_recv()
            acc[...] += dot(hin[q, k], wd[k, q * FH : (q + 1) * FH])

    rr = xs

    def send5(k, h, at):
        return pltpu.make_async_remote_copy(
            rr.at[h, block(k)], back.at[h, block(at)], s5.at[k, h], r5.at[k, h],
            device_id=(mb, expert_at(-k)), device_id_type=MESH,
        )

    send4(B - 1, G - 1).wait_recv()
    for h in range(H):
        for k in range(1, E):
            send2(k, h).wait_send()
        cols = slice(h * DH, (h + 1) * DH)
        rows = acc[:, cols] + dot(hin[G - 1, B - 1], wd[B - 1, (G - 1) * FH : G * FH, cols])
        rr[h] = dot(p2t[...], rows.astype(BF)).astype(BF)
        for k in range(1, E):
            send5(k, h, me).start()
        back[h, block(me)] = rr[h, 0:RP]

    def send6(k, h, at):
        return pltpu.make_async_remote_copy(
            rb.at[k, h], fin.at[at, h], s6.at[k, h], r6.at[k, h],
            device_id=(bulk_at(k), me), device_id_type=MESH,
        )

    def keep(h):
        return pltpu.make_async_copy(rb.at[0, h], fin.at[mb, h], fsem.at[h])

    for h in range(H):
        for k in range(1, E):
            send5(k, h, expert_at(k)).wait_recv()
        for k in order:
            rb[k, h] = dot(p1t[bulk_at(k)], back[h]).astype(BF)
            if k:
                send6(k, h, mb).start()
            else:
                keep(h).start()
    for copy in side:
        copy.wait()
    for k in range(1, B):
        for h in range(H):
            send1(k, h).wait_send()
            send6(k, h, mb).wait_send()
        for q in range(G):
            direct(bulk_at(k), q).wait_send()
            send4(k, q).wait_send()
    for k in range(1, E):
        for h in range(H):
            send5(k, h, me).wait_send()
    for h in range(H):
        keep(h).wait()
        for k in range(1, B):
            send6(k, h, bulk_at(-k)).wait_recv()


def combine_kernel(fin, cs, ld, out_hbm, load, out, sems):
    B, H, SL, DH = fin.shape
    load[...] = ld[:1].astype(jnp.int32)
    copies = []
    for b in range(B):
        for h in range(H):
            rows = fin[b, h]
            at = (b * H + h) * DH
            out[:, at : at + DH] = (
                dot(cs[0], rows) + (dot(cs[1], rows) + dot(cs[2], rows))
            ).astype(BF)
        cols = pl.ds(b * H * DH, H * DH)
        copies.append(pltpu.make_async_copy(out.at[:, cols], out_hbm.at[:, cols], sems.at[b]))
        copies[-1].start()
    for copy in copies:
        copy.wait()


def on_device(tokens, expert_ids, gate_values, placement, gate_weight, up_weight, down_weight):
    E = lax.axis_size("expert")
    B = lax.axis_size("bulk")
    T, D = tokens.shape
    DS = gate_weight.shape[1]
    FB = gate_weight.shape[2] // B
    SL = E * CAP
    RQ = B * CAP
    RP = -(-RQ // 16) * 16
    R = E * RQ
    p1 = np.zeros((B, E * RP, SL), np.float32)
    p2 = np.zeros((R, E * RP), np.float32)
    for e in range(E):
        for q in range(RQ):
            p1[q // CAP, e * RP + q, e * CAP + q % CAP] = 1.0
            p2[e * RQ + q, e * RP + q] = 1.0
    p1t = np.swapaxes(p1, 1, 2)
    consts = [jnp.asarray(a.astype(ml_dtypes.bfloat16)) for a in (p1, p1t, p2, p2.T)]
    H = 2 if DS % 256 == 0 else 1
    G = 2 if FB % 256 == 0 else 1
    DH = DS // H
    FH = FB // G
    vmem = pl.BlockSpec(memory_space=pltpu.VMEM)
    hbm = pl.BlockSpec(memory_space=pl.ANY)
    dma = pltpu.SemaphoreType.DMA
    buffers = [
        (T, D), (B, DS, FB), (B, DS, FB), (B, FB, DS),
        (B, H, SL, DH), (B, H, SL, DH), (H, E * RP, DH), (H, E * RP, DH), (R, DS),
        (G, B, R, 2 * FH), (G, B + B // 2, R, 2 * FH), (G, B, R, FH), (R, DS),
        (H, E * RP, DH), (B, H, SL, DH), (3, T, SL), (8, E),
    ]
    sems = [(B, H), (B, H), (E, H), (E, H)] + [(B, G), (B + B // 2, G), (B, G), (B, G)] + [(E, H), (E, H), (B, H), (B, H)]
    fin, cs, ld = pl.pallas_call(
        functools.partial(kernel, B, E, RP, H, G),
        out_shape=(
            jax.ShapeDtypeStruct((B, H, SL, DH), BF),
            jax.ShapeDtypeStruct((3, T, SL), BF),
            jax.ShapeDtypeStruct((8, E), F32),
        ),
        in_specs=[hbm] + [vmem] * 7 + [hbm] * 3,
        out_specs=(hbm, hbm, hbm),
        scratch_shapes=[pltpu.VMEM(d, F32 if i in (12, 16) else BF) for i, d in enumerate(buffers)]
        + [dma, dma((2,)), dma((H,)), dma((3, B))]
        + [dma(n) for n in sems],
        compiler_params=pltpu.CompilerParams(
            collective_id=0, has_side_effects=True, vmem_limit_bytes=62 * 1024 * 1024
        ),
    )(tokens, expert_ids.T, gate_values.T, placement.reshape(1, E), *consts,
      gate_weight, up_weight, down_weight)
    return pl.pallas_call(
        combine_kernel,
        out_shape=(
            jax.ShapeDtypeStruct((T, D), BF),
            jax.ShapeDtypeStruct((1, E), jnp.int32),
        ),
        in_specs=[vmem] * 3,
        out_specs=(hbm, vmem),
        scratch_shapes=[pltpu.VMEM((T, D), BF), dma((B,))],
    )(fin, cs, ld)


def solution(mesh):
    placed = (
        P(("bulk", "expert"), None),
        P(("bulk", "expert"), None),
        P(("bulk", "expert"), None),
        P(),
        P("expert", "bulk", None),
        P("expert", "bulk", None),
        P("expert", None, "bulk"),
    )
    return jax.shard_map(
        on_device,
        mesh=mesh,
        in_specs=placed,
        out_specs=(P(("bulk", "expert"), None), P(("bulk", "expert"), None)),
        check_vma=False,
    )
```

```python
import functools

import jax
import jax.numpy as jnp
import ml_dtypes
import numpy as np
from jax import lax
from jax.experimental import pallas as pl
from jax.experimental.pallas import tpu as pltpu
from jax.sharding import PartitionSpec as P

CAP = 3
BF = jnp.bfloat16
F32 = jnp.float32
MESH = pl.DeviceIdType.MESH


def dot(a, b):
    return jnp.dot(a, b, preferred_element_type=F32)


def kernel(
    B, E, RP, H, G, tok_hbm, ids, gv, place, p1, p1t, p2, p2t, wg_hbm, wu_hbm, wd_hbm,
    fin, cs, ld, tok, wg, wu, wd, og, oin, xs, xr, x, pout, pin, hin, acc, back, rb, csv, ldv,
    tsem, csem, fsem, wsem, s1, r1, s2, r2, s3, r3, s4, r4, s5, r5, s6, r6,
):
    TOP, T = ids.shape
    SL = E * CAP
    DS = wg_hbm.shape[1]
    FB = wg_hbm.shape[2] // B
    DH = DS // H
    FH = FB // G
    mb = lax.axis_index("bulk")
    me = lax.axis_index("expert")

    def bulk_at(k):
        return lax.rem(mb + k + B, B)

    def expert_at(k):
        return lax.rem(me + k + E, E)

    def weight_copy(i, k):
        if i == 2:
            rows = pl.ds(pl.multiple_of(bulk_at(-k) * FB, FB), FB)
            return pltpu.make_async_copy(wd_hbm.at[0, rows, :], wd.at[k], wsem.at[2, k])
        cols = pl.ds(pl.multiple_of(bulk_at(k) * FB, FB), FB)
        source, to = ((wg_hbm, wg), (wu_hbm, wu))[i]
        return pltpu.make_async_copy(source.at[0, :, cols], to.at[k], wsem.at[i, k])

    tok_copy = pltpu.make_async_copy(tok_hbm, tok, tsem)
    tok_copy.start()
    far_first = [(i + B // 2 - 1) % (B - 1) + 1 for i in range(B - 1)]
    order = far_first + [0]
    barrier = pltpu.get_barrier_semaphore()
    for k in range(1, B):
        pl.semaphore_signal(barrier, inc=1, device_id=(bulk_at(k), me), device_id_type=MESH)
    for k in range(1, E):
        pl.semaphore_signal(barrier, inc=1, device_id=(mb, expert_at(k)), device_id_type=MESH)

    slot = lax.broadcasted_iota(jnp.int32, (SL, T), 0)
    slot_expert = lax.div(slot, CAP)
    slot_rank = slot - slot_expert * CAP
    named = jnp.zeros((SL, T), F32)
    gates = jnp.zeros((SL, T), F32)
    for j in range(TOP):
        hit = ids[j : j + 1, :] == slot_expert
        named = named + jnp.where(hit, 1.0, 0.0)
        gates = gates + jnp.where(hit, gv[j : j + 1, :], 0.0)
    t_row = lax.broadcasted_iota(jnp.int32, (T, T), 0)
    t_col = lax.broadcasted_iota(jnp.int32, (T, T), 1)
    before = jnp.where(t_row < t_col, 1.0, 0.0).astype(BF)
    rank = dot(named.astype(BF), before)
    chosen = jnp.where(rank == slot_rank.astype(F32), named, 0.0)
    selector = chosen.astype(BF)

    def send1(k, h):
        return pltpu.make_async_remote_copy(
            og.at[k, h], oin.at[k, h], s1.at[k, h], r1.at[k, h],
            device_id=(bulk_at(k), me), device_id_type=MESH,
        )

    pl.semaphore_wait(barrier, B + E - 2)
    tok_copy.wait()
    for h in range(H):
        for k in order:
            cols = pl.ds(pl.multiple_of(bulk_at(k) * DS + h * DH, 128), DH)
            rows = dot(selector, tok[:, cols]).astype(BF)
            if k:
                og[k, h] = rows
                send1(k, h).start()
            else:
                oin[0, h] = rows
    for k in order:
        weight_copy(0, k).start()
        weight_copy(1, k).start()
    for k in range(B):
        weight_copy(2, k).start()

    member = jnp.zeros((E, T), F32)
    e_iota = lax.broadcasted_iota(jnp.int32, (E, T), 0)
    for j in range(TOP):
        member = member + jnp.where(ids[j : j + 1, :] == e_iota, 1.0, 0.0)
    odd_t = lax.rem(lax.broadcasted_iota(jnp.int32, (8, T), 1), 2) == 1
    odd = jnp.where(odd_t, 1.0, 0.0).astype(BF)
    even = jnp.where(odd_t, 0.0, 1.0).astype(BF)
    er = lax.broadcasted_iota(jnp.int32, (E, E), 0)
    ec = lax.broadcasted_iota(jnp.int32, (E, E), 1)
    shift = jnp.where(er == lax.rem(ec + 1, E), 1.0, 0.0).astype(BF)
    home = jnp.where(er == place[...], 1.0, 0.0).astype(BF)

    def across(a, b):
        return lax.dot_general(a, b, (((1,), (1,)), ((), ())), preferred_element_type=F32)

    member = member.astype(BF)
    loads = across(across(odd, member).astype(BF), shift) + across(
        across(even, member).astype(BF), home
    )
    ldv[...] = loads
    eye = jnp.where(t_row == t_col, 1.0, 0.0).astype(BF)
    combine = chosen * gates
    c_hi = combine.astype(BF)
    c_rest = combine - c_hi.astype(F32)
    c_mid = c_rest.astype(BF)
    c_lo = (c_rest - c_mid.astype(F32)).astype(BF)
    for i, c in enumerate((c_hi, c_mid, c_lo)):
        csv[i] = across(eye, c).astype(BF)
    side = (
        pltpu.make_async_copy(csv, cs, csem.at[0]),
        pltpu.make_async_copy(ldv, ld, csem.at[1]),
    )
    for copy in side:
        copy.start()

    def block(k):
        return pl.ds(pl.multiple_of(k * RP, RP), RP)

    def send2(k, h):
        return pltpu.make_async_remote_copy(
            xs.at[h, block(expert_at(k))], xr.at[h, block(k)], s2.at[k, h], r2.at[k, h],
            device_id=(mb, expert_at(k)), device_id_type=MESH,
        )

    for h in range(H):
        rows = dot(p1[mb], oin[0, h])
        for k in range(1, B):
            send1(k, h).wait_recv()
            rows = rows + dot(p1[bulk_at(-k)], oin[k, h])
        xs[h] = rows.astype(BF)
        for k in range(1, E):
            send2(k, h).start()
        xr[h, 0:RP] = xs[h, block(me)]
    for h in range(H):
        for k in range(1, E):
            send2(k, h).wait_recv()
        x[:, h * DH : (h + 1) * DH] = dot(p2[...], xr[h]).astype(BF)

    pair = lax.div(mb, 2)
    is_odd = lax.rem(mb, 2)
    partner = mb + 1 - 2 * is_odd

    def direct(d, q):
        return pltpu.make_async_remote_copy(
            pout.at[q, d], pin.at[q, pair], s3.at[d, q], r3.at[pair, q],
            device_id=(d, me), device_id_type=MESH,
        )

    def relay(d, q):
        return pltpu.make_async_remote_copy(
            pout.at[q, d], pin.at[q, B // 2 + d], s3.at[d, q], r3.at[B // 2 + d, q],
            device_id=(partner, me), device_id_type=MESH,
        )

    def arrival(p, q):
        return pltpu.make_async_remote_copy(
            pout.at[q, mb], pin.at[q, p], s3.at[mb, q], r3.at[p, q],
            device_id=(partner, me), device_id_type=MESH,
        )

    def above(d):
        return jnp.where(lax.div(d, 2) > pair, 1, 0)

    def partials(d, k, q):
        cols = slice(q * FH, (q + 1) * FH)
        pout[q, d, :, :FH] = dot(x[...], wg[k, :, cols]).astype(BF)
        pout[q, d, :, FH:] = dot(x[...], wu[k, :, cols]).astype(BF)

    for q in range(G):

        @pl.loop(0, B - 1)
        def _(i):
            d = jnp.where(i < B - 2, lax.rem(2 * pair + 2 + i, B), partner)
            k = lax.rem(d - mb + B, B)
            if q == 0:
                weight_copy(0, k).wait()
                weight_copy(1, k).wait()
            partials(d, k, q)

            @pl.when(d == partner)
            def _():
                direct(d, q).start()

            @pl.when((d != partner) & (above(d) != is_odd))
            def _():
                relay(d, q).start()

    weight_copy(0, 0).wait()
    weight_copy(1, 0).wait()
    for q in range(G):
        partials(mb, 0, q)

    for q in range(G):

        @pl.loop(0, B - 1)
        def _(i):
            d = jnp.where(i < B - 2, lax.rem(2 * pair + 2 + i, B), partner)

            @pl.when((d != partner) & (above(d) == is_odd))
            def _():
                arrival(B // 2 + d, q).wait_recv()
                both = pout[q, d].astype(F32) + pin[q, B // 2 + d].astype(F32)
                pout[q, d] = both.astype(BF)
                direct(d, q).start()

    def send4(k, q):
        return pltpu.make_async_remote_copy(
            hin.at[q, 0], hin.at[q, k], s4.at[k, q], r4.at[k, q],
            device_id=(bulk_at(k), me), device_id_type=MESH,
        )

    for q in range(G):
        total = pout[q, mb].astype(F32)
        for p in range(B // 2):
            arrival(p, q).wait_recv()
            total = total + pin[q, p].astype(F32)
        gate = total[:, :FH]
        hin[q, 0] = (gate / (1.0 + jnp.exp(-gate)) * total[:, FH:]).astype(BF)
        for k in far_first:
            send4(k, q).start()
    weight_copy(2, 0).wait()
    acc[...] = dot(hin[0, 0], wd[0, 0:FH])
    for q in range(1, G):
        acc[...] += dot(hin[q, 0], wd[0, q * FH : (q + 1) * FH])
    for k in range(1, B):
        weight_copy(2, k).wait()
    for q in range(G):

        @pl.loop(1, B - 1 if q == G - 1 else B)
        def _(k):
            send4(k, q).wait_recv()
            acc[...] += dot(hin[q, k], wd[k, q * FH : (q + 1) * FH])

    rr = xs

    def send5(k, h, at):
        return pltpu.make_async_remote_copy(
            rr.at[h, block(k)], back.at[h, block(at)], s5.at[k, h], r5.at[k, h],
            device_id=(mb, expert_at(-k)), device_id_type=MESH,
        )

    send4(B - 1, G - 1).wait_recv()
    for h in range(H):
        for k in range(1, E):
            send2(k, h).wait_send()
        cols = slice(h * DH, (h + 1) * DH)
        rows = acc[:, cols] + dot(hin[G - 1, B - 1], wd[B - 1, (G - 1) * FH : G * FH, cols])
        rr[h] = dot(p2t[...], rows.astype(BF)).astype(BF)
        for k in range(1, E):
            send5(k, h, me).start()
        back[h, block(me)] = rr[h, 0:RP]

    def send6(k, h, at):
        return pltpu.make_async_remote_copy(
            rb.at[k, h], fin.at[at, h], s6.at[k, h], r6.at[k, h],
            device_id=(bulk_at(k), me), device_id_type=MESH,
        )

    def keep(h):
        return pltpu.make_async_copy(rb.at[0, h], fin.at[mb, h], fsem.at[h])

    for h in range(H):
        for k in range(1, E):
            send5(k, h, expert_at(k)).wait_recv()
        for k in order:
            rb[k, h] = dot(p1t[bulk_at(k)], back[h]).astype(BF)
            if k:
                send6(k, h, mb).start()
            else:
                keep(h).start()
    for copy in side:
        copy.wait()
    for k in range(1, B):
        for h in range(H):
            send1(k, h).wait_send()
            send6(k, h, mb).wait_send()
        for q in range(G):
            direct(bulk_at(k), q).wait_send()
            send4(k, q).wait_send()
    for k in range(1, E):
        for h in range(H):
            send5(k, h, me).wait_send()
    for h in range(H):
        keep(h).wait()
        for k in range(1, B):
            send6(k, h, bulk_at(-k)).wait_recv()


def combine_kernel(fin, cs, ld, out_hbm, load, out, sems):
    B, H, SL, DH = fin.shape
    load[...] = ld[:1].astype(jnp.int32)
    copies = []
    for b in range(B):
        for h in range(H):
            rows = fin[b, h]
            at = (b * H + h) * DH
            out[:, at : at + DH] = (
                dot(cs[0], rows) + (dot(cs[1], rows) + dot(cs[2], rows))
            ).astype(BF)
        cols = pl.ds(b * H * DH, H * DH)
        copies.append(pltpu.make_async_copy(out.at[:, cols], out_hbm.at[:, cols], sems.at[b]))
        copies[-1].start()
    for copy in copies:
        copy.wait()


def on_device(tokens, expert_ids, gate_values, placement, gate_weight, up_weight, down_weight):
    E = lax.axis_size("expert")
    B = lax.axis_size("bulk")
    T, D = tokens.shape
    DS = gate_weight.shape[1]
    FB = gate_weight.shape[2] // B
    SL = E * CAP
    RQ = B * CAP
    RP = -(-RQ // 16) * 16
    R = E * RQ
    p1 = np.zeros((B, E * RP, SL), np.float32)
    p2 = np.zeros((R, E * RP), np.float32)
    for e in range(E):
        for q in range(RQ):
            p1[q // CAP, e * RP + q, e * CAP + q % CAP] = 1.0
            p2[e * RQ + q, e * RP + q] = 1.0
    p1t = np.swapaxes(p1, 1, 2)
    consts = [jnp.asarray(a.astype(ml_dtypes.bfloat16)) for a in (p1, p1t, p2, p2.T)]
    H = 2 if DS % 256 == 0 else 1
    G = 2 if FB % 256 == 0 else 1
    DH = DS // H
    FH = FB // G
    vmem = pl.BlockSpec(memory_space=pltpu.VMEM)
    hbm = pl.BlockSpec(memory_space=pl.ANY)
    dma = pltpu.SemaphoreType.DMA
    buffers = [
        (T, D), (B, DS, FB), (B, DS, FB), (B, FB, DS),
        (B, H, SL, DH), (B, H, SL, DH), (H, E * RP, DH), (H, E * RP, DH), (R, DS),
        (G, B, R, 2 * FH), (G, B + B // 2, R, 2 * FH), (G, B, R, FH), (R, DS),
        (H, E * RP, DH), (B, H, SL, DH), (3, T, SL), (8, E),
    ]
    sems = [(B, H), (B, H), (E, H), (E, H)] + [(B, G), (B + B // 2, G), (B, G), (B, G)] + [(E, H), (E, H), (B, H), (B, H)]
    fin, cs, ld = pl.pallas_call(
        functools.partial(kernel, B, E, RP, H, G),
        out_shape=(
            jax.ShapeDtypeStruct((B, H, SL, DH), BF),
            jax.ShapeDtypeStruct((3, T, SL), BF),
            jax.ShapeDtypeStruct((8, E), F32),
        ),
        in_specs=[hbm] + [vmem] * 7 + [hbm] * 3,
        out_specs=(hbm, hbm, hbm),
        scratch_shapes=[pltpu.VMEM(d, F32 if i in (12, 16) else BF) for i, d in enumerate(buffers)]
        + [dma, dma((2,)), dma((H,)), dma((3, B))]
        + [dma(n) for n in sems],
        compiler_params=pltpu.CompilerParams(
            collective_id=0, has_side_effects=True, vmem_limit_bytes=62 * 1024 * 1024
        ),
    )(tokens, expert_ids.T, gate_values.T, placement.reshape(1, E), *consts,
      gate_weight, up_weight, down_weight)
    return pl.pallas_call(
        combine_kernel,
        out_shape=(
            jax.ShapeDtypeStruct((T, D), BF),
            jax.ShapeDtypeStruct((1, E), jnp.int32),
        ),
        in_specs=[vmem] * 3,
        out_specs=(hbm, vmem),
        scratch_shapes=[pltpu.VMEM((T, D), BF), dma((B,))],
    )(fin, cs, ld)


def solution(mesh):
    placed = (
        P(("bulk", "expert"), None),
        P(("bulk", "expert"), None),
        P(("bulk", "expert"), None),
        P(),
        P("expert", "bulk", None),
        P("expert", "bulk", None),
        P("expert", None, "bulk"),
    )
    return jax.shard_map(
        on_device,
        mesh=mesh,
        in_specs=placed,
        out_specs=(P(("bulk", "expert"), None), P(("bulk", "expert"), None)),
        check_vma=False,
    )
```
